32 devices in a mesh: dp: 8 (over z, x), tensor: 4 (over y, core).
Axes of the slice: x: 2, y: 2, z: 4, core: 2. Of those that a mesh axis runs over, the one named last changes fastest.
Arguments:
- tokens: bfloat16 [24576, 768], P('dp'), may hold values from -6 to 6
- cotangent: bfloat16 [24576, 768], P('dp'), may hold values from -6 to 6
- doc_lengths: int32 [8, 6], P('dp'), may hold values from 0 to 1536, as said below
- qkv_weight: bfloat16 [3, 768, 768], P(None, None, 'tensor'), may hold values from -0.21875 to 0.21875
- qkv_bias: float32 [3, 768], P(None, 'tensor'), may hold values from -3 to 3
- out_weight: bfloat16 [768, 768], P('tensor'), may hold values from -2 to 2
- out_bias: float32 [768], replicated, may hold values from -3 to 3
- up_weight: bfloat16 [768, 3072], P(None, 'tensor'), may hold values from -0.21875 to 0.21875
- up_bias: float32 [3072], P('tensor'), may hold values from -3 to 3
- down_weight: bfloat16 [3072, 768], P('tensor'), may hold values from -0.109375 to 0.109375
- down_bias: float32 [768], replicated, may hold values from -3 to 3
- norm_gains: float32 [2, 768], replicated, may hold values from 0.5 to 1.5
- norm_shifts: float32 [2, 768], replicated, may hold values from -3 to 3
Outputs:
- output: bfloat16 [24576, 768], P('dp')
- input_grad: float32 [24576, 768], P('dp')
- qkv_weight_grad: float32 [3, 768, 768], P(None, None, 'tensor')
- qkv_bias_grad: float32 [3, 768], P(None, 'tensor')
- out_weight_grad: float32 [768, 768], P('tensor')
- out_bias_grad: float32 [768], replicated
- up_weight_grad: float32 [768, 3072], P(None, 'tensor')
- up_bias_grad: float32 [3072], P('tensor')
- down_weight_grad: float32 [3072, 768], P('tensor')
- down_bias_grad: float32 [768], replicated
- norm_gains_grad: float32 [2, 768], replicated
- norm_shifts_grad: float32 [2, 768], replicated
The draws below stay inside these ranges and needn't reach their ends.
Inputs may be any that keep to these rules, and one draw needn't show every extreme that they name: `doc_lengths`: each row lists, in order, the lengths of the sequences of one index of dp: multiples of 512 of at most 1536, summing to 3072; zeros follow the last sequence.
All inputs are finite; a program needn't handle non-finite values.
Results may differ from the reference program's by a relative error of at most 0.022.
Values may be sent and summed in bfloat16 or wider, within the bound.
No kernel may reach another device: no remote copies, remote signals or barrier semaphores. Data moves between devices by JAX's collectives and lax.ppermute only.
A program may use at most 128 MiB of HBM per device.

```python
import math
import jax
import jax.numpy as jnp
from jax import lax

D = 768
HEADS = 12
HD = 64
FF = 3072
BLK = 512
WINDOW = 3
BLOCKS_DEV = 6
TOK_DEV = 3072
GROUPS = 8
TOKENS = 24576
N_TENSOR = 4


def draw_doc_lengths(key, part):
    key_len, key_row = jax.random.split(jax.random.fold_in(key, 17))
    pieces = jax.random.randint(key_len, (GROUPS, BLOCKS_DEV), 1, WINDOW + 1).astype(jnp.int32)
    chosen = jax.random.randint(key_row, (), 0, GROUPS).astype(jnp.int32)
    rows = jnp.arange(GROUPS, dtype=jnp.int32)
    leading = jnp.where(rows == chosen, WINDOW, pieces[:, 0]).astype(jnp.int32)
    pieces = pieces.at[:, 0].set(leading)
    before = (jnp.cumsum(pieces, axis=1) - pieces).astype(jnp.int32)
    kept = jnp.clip(BLOCKS_DEV - before, 0, pieces)
    return (kept * BLK).astype(jnp.int32)


def block_levels(rng, shape, cuts, low, largest):
    def one(position, parts):
        heights = jax.random.uniform(jax.random.fold_in(jax.random.fold_in(rng, 6), position), (parts,), jnp.float32, low / len(cuts), largest / len(cuts))
        return jnp.repeat(jnp.exp(heights), shape[position] // parts).reshape((-1,) + (1,) * (len(shape) - position - 1))

    level = one(*cuts[0])
    for cut in cuts[1:]:
        level = level * one(*cut)
    return level


def noise(own_key, dims, scale, bound, cuts=(), held_as=jnp.bfloat16):
    values = scale * jax.random.normal(own_key, dims, jnp.float32)
    if cuts:
        values = values * block_levels(own_key, dims, cuts, -0.22, 0.18)
    return jnp.clip(values, -bound, bound).astype(held_as)


def setup_inputs(seed: int = 0) -> dict:
    key_of = jax.random.split(jax.random.key(seed), 14)
    tokens = noise(key_of[0], (TOKENS, D), 1.0, 6.0, ((0, 8),))
    cotangent = noise(key_of[1], (TOKENS, D), 1.0, 6.0, ((0, 8),))
    doc_lengths = draw_doc_lengths(jax.random.fold_in(key_of[13], 71), 0)
    qkv_weight = noise(key_of[3], (3, D, HEADS * HD), D ** -0.5, 0.21875, ((2, 4),))
    qkv_bias = noise(key_of[4], (3, HEADS * HD), 0.5, 3.0, ((1, 4),), jnp.float32)
    out_weight = noise(key_of[5], (HEADS * HD, D), (HD // 8) ** -0.5, 2.0, ((0, 4),))
    out_bias = noise(key_of[6], (D,), 0.5, 3.0, (), jnp.float32)
    up_weight = noise(key_of[7], (D, FF), D ** -0.5, 0.21875, ((1, 4),))
    up_bias = noise(key_of[8], (FF,), 0.5, 3.0, ((0, 4),), jnp.float32)
    down_weight = noise(key_of[9], (FF, D), FF ** -0.5, 0.109375, ((0, 4),))
    down_bias = noise(key_of[10], (D,), 0.5, 3.0, (), jnp.float32)
    norm_gains = jnp.clip(1.0 + 0.1 * jax.random.normal(key_of[11], (2, D), jnp.float32), 0.5, 1.5)
    norm_shifts = noise(key_of[12], (2, D), 0.5, 3.0, (), jnp.float32)
    return dict(tokens=tokens, cotangent=cotangent, doc_lengths=doc_lengths, qkv_weight=qkv_weight, qkv_bias=qkv_bias, out_weight=out_weight, out_bias=out_bias, up_weight=up_weight, up_bias=up_bias, down_weight=down_weight, down_bias=down_bias, norm_gains=norm_gains, norm_shifts=norm_shifts)


@jax.custom_vjp
def low(v):
    return lax.optimization_barrier(v.astype(jnp.bfloat16)).astype(jnp.float32)

@jax.custom_vjp
def low_back(v):
    return v

def low_keep(v):
    return (low(v), None)

def low_pass(kept, grad):
    return (grad,)

def back_keep(v):
    return (v, None)

def back_low(kept, grad):
    return (low(grad),)
low.defvjp(low_keep, low_pass)
low_back.defvjp(back_keep, back_low)

def rotate(values, cosine, sine):
    half = values.shape[-1] // 2
    first = values[..., :half]
    second = values[..., half:]
    return jnp.concatenate([first * cosine - second * sine, second * cosine + first * sine], axis=-1)

def layer_norm(values, gain, shift):
    mean = lax.optimization_barrier(jnp.mean(values, axis=-1, keepdims=True))
    centred = values - mean
    spread = lax.optimization_barrier(jnp.mean(centred * centred, axis=-1, keepdims=True))
    return centred * lax.rsqrt(spread + 1e-05) * gain + shift

def gelu_value(values):
    return 0.5 * values * (1.0 + lax.erf(values * 0.7071067811865476))

def group_layer(params, tokens, lengths):
    qkv_w, qkv_b, out_w, out_b, up_w, up_b, down_w, down_b, gains, shifts = params
    highest = lax.Precision.HIGHEST
    rows = tokens.shape[0]
    lengths = lengths.astype(jnp.int32)
    ends = jnp.cumsum(lengths).astype(jnp.int32)
    index = jnp.arange(rows, dtype=jnp.int32)
    after = index[:, None] >= ends[None, :]
    segment = lax.optimization_barrier(jnp.sum(after.astype(jnp.int32), axis=1)).astype(jnp.int32)
    begin = lax.optimization_barrier(jnp.sum(jnp.where(after, lengths[None, :], 0), axis=1)).astype(jnp.int32)
    place = (index - begin).astype(jnp.float32)
    freqs = jnp.exp(jnp.arange(HD // 2, dtype=jnp.float32) * (-2.0 * math.log(10000.0) / HD))
    angle = place[:, None] * freqs[None, :]
    cosine = jnp.cos(angle)[:, None, :]
    sine = jnp.sin(angle)[:, None, :]
    width = HEADS * HD // N_TENSOR
    fwidth = FF // N_TENSOR
    pieces = []
    for group in range(N_TENSOR):
        part_x = low_back(tokens)
        weight_cols = qkv_w[:, :, group * width:(group + 1) * width]
        pieces.append(low_back(jnp.einsum('td,cde->cte', part_x, weight_cols, precision=highest)))
    projected = jnp.concatenate(pieces, axis=2) + qkv_b[:, None, :]
    shape3 = (rows, HEADS, HD)
    queries = low(rotate(projected[0].reshape(shape3), cosine, sine))
    keys = low(rotate(projected[1].reshape(shape3), cosine, sine))
    values = low(projected[2].reshape(shape3))
    span = WINDOW * BLK
    anchors = jnp.minimum(begin.reshape(rows // BLK, BLK)[:, 0], rows - span).astype(jnp.int32)
    scale = HD ** (-0.5)

    def attend(pair):
        block, anchor = pair
        query = lax.dynamic_slice_in_dim(queries, block * BLK, BLK, 0)
        near = lax.dynamic_slice_in_dim(keys, anchor, span, 0)
        vals = lax.dynamic_slice_in_dim(values, anchor, span, 0)
        seg_q = lax.dynamic_slice_in_dim(segment, block * BLK, BLK, 0)
        seg_k = lax.dynamic_slice_in_dim(segment, anchor, span, 0)
        scores = low_back(jnp.einsum('qhd,khd->hqk', query, near, precision=highest) * scale)
        scores = jnp.where((seg_q[:, None] == seg_k[None, :])[None], scores, -1e+30)
        peak = lax.optimization_barrier(jnp.max(scores, axis=-1, keepdims=True))
        expo = jnp.exp(scores - peak)
        probs = expo / lax.optimization_barrier(jnp.sum(expo, axis=-1, keepdims=True))
        mixed = jnp.einsum('hqk,khd->qhd', low(probs), vals, precision=highest)
        return low(low_back(mixed))
    blocks = jnp.arange(rows // BLK, dtype=jnp.int32)
    mixed = lax.map(jax.checkpoint(attend), (blocks, anchors)).reshape(rows, HEADS * HD)
    attn_total = jnp.zeros((rows, D), jnp.float32)
    for group in range(N_TENSOR):
        cols = mixed[:, group * width:(group + 1) * width]
        attn_total = attn_total + low(jnp.dot(cols, out_w[group * width:(group + 1) * width, :], precision=highest))
    first_sum = tokens + low_back(attn_total) + out_b
    hidden = layer_norm(first_sum, gains[0], shifts[0])
    hidden_low = low(hidden)
    ffn_total = jnp.zeros((rows, D), jnp.float32)
    for group in range(N_TENSOR):
        part_h = low_back(hidden_low)
        pre = low_back(jnp.dot(part_h, up_w[:, group * fwidth:(group + 1) * fwidth], precision=highest)) + up_b[group * fwidth:(group + 1) * fwidth]
        active = low(gelu_value(pre))
        ffn_total = ffn_total + low(jnp.dot(active, down_w[group * fwidth:(group + 1) * fwidth, :], precision=highest))
    second_sum = hidden + low_back(ffn_total) + down_b
    return layer_norm(second_sum, gains[1], shifts[1])

def reference(tokens, cotangent, doc_lengths, qkv_weight, qkv_bias, out_weight, out_bias, up_weight, up_bias, down_weight, down_bias, norm_gains, norm_shifts):
    params = (qkv_weight.astype(jnp.float32), qkv_bias.astype(jnp.float32), out_weight.astype(jnp.float32), out_bias.astype(jnp.float32), up_weight.astype(jnp.float32), up_bias.astype(jnp.float32), down_weight.astype(jnp.float32), down_bias.astype(jnp.float32), norm_gains.astype(jnp.float32), norm_shifts.astype(jnp.float32))
    inputs = tokens.astype(jnp.float32).reshape(GROUPS, TOK_DEV, D)

    def forward(weights, acts):

        def one_group(pair):
            return jax.checkpoint(group_layer)(weights, pair[0], pair[1])
        return lax.map(one_group, (acts, doc_lengths))
    result, pull = jax.vjp(forward, params, inputs)
    grads, input_grad = pull(cotangent.astype(jnp.float32).reshape(GROUPS, TOK_DEV, D))
    factor = 1.0 / math.sqrt(TOKENS)
    return (result.reshape(TOKENS, D).astype(jnp.bfloat16), input_grad.reshape(TOKENS, D), grads[0] * factor, grads[1] * factor, grads[2] * factor, grads[3] * factor, grads[4] * factor, grads[5] * factor, grads[6] * factor, grads[7] * factor, grads[8] * factor, grads[9] * factor)
```

```python
import functools
import math

import jax
import jax.numpy as jnp
import numpy as np
from jax import lax
from jax.experimental import pallas as pl
from jax.experimental.pallas import tpu as pltpu
from jax.sharding import PartitionSpec as P

HD = 64
HALF = HD // 2
BLK = 512
WINDOW = 3
SPAN = WINDOW * BLK
TILE = 256
NC = 2
LOW = jnp.bfloat16
F32 = jnp.float32


def contract(a, b, ca, cb):
    return lax.dot_general(a, b, (((ca,), (cb,)), ((), ())), preferred_element_type=F32)


def trig_table():
    freqs = np.exp(np.arange(HALF) * (-2.0 * math.log(10000.0) / HD))
    angle = freqs[:, None] * np.arange(SPAN)[None, :]
    return np.concatenate([np.cos(angle), np.sin(angle)], axis=0).astype(np.float32)


def normalize(values):
    mean = jnp.mean(values, axis=-1, keepdims=True)
    centred = values - mean
    inverse = lax.rsqrt(jnp.mean(centred * centred, axis=-1, keepdims=True) + 1e-05)
    return (centred * inverse, inverse)


def normalize_back(grad_out, unit, inverse, gain):
    scaled = grad_out * gain
    return inverse * (
        scaled
        - jnp.mean(scaled, axis=-1, keepdims=True)
        - unit * jnp.mean(scaled * unit, axis=-1, keepdims=True)
    )


def gelu_value(values):
    return 0.5 * values * (1.0 + lax.erf(values * 0.7071067811865476))


def gelu_slope(values):
    return (
        0.5 * (1.0 + lax.erf(values * 0.7071067811865476))
        + values * jnp.exp(-0.5 * values * values) * 0.3989422804014327
    )


def bounds_of(len_ref, count, block):
    row = block * BLK
    start = jnp.int32(0)
    size = jnp.int32(0)
    total = jnp.int32(0)
    for i in range(count):
        length = len_ref[i]
        inside = (row >= total) & (row < total + length)
        start = jnp.where(inside, total, start)
        size = jnp.where(inside, length, size)
        total = total + length
    return start, size // BLK


def forward_kernel(
    count,
    len_ref,
    pos_ref,
    tok_ref,
    w_ref,
    b_ref,
    trig_ref,
    qkv_ref,
    pt_ref,
    ot_ref,
    r_ref,
    m0,
    m1,
    m2,
    m3,
    wt,
    bias,
    s_scr,
    mix,
):
    block = pl.program_id(0)
    blocks = pl.num_programs(0)
    rows = tok_ref.shape[0]
    cols = w_ref.shape[2]
    heads = cols // HD
    piece = rows // (NC * 4)

    @pl.when(block == 0)
    def _():
        for c in range(3):
            wt[c * cols : (c + 1) * cols, :] = w_ref[c].T
            bias[c * cols : (c + 1) * cols, :] = jnp.broadcast_to(b_ref[c : c + 1, :], (128, cols)).T

        def project(j, carry):
            start, _ = bounds_of(len_ref, count, j)
            off = pl.multiple_of(j * BLK - start, BLK)
            at = pl.ds(pl.multiple_of(j * BLK, BLK), BLK)
            cosine = trig_ref[0:HALF, pl.ds(off, BLK)]
            sine = trig_ref[HALF:HD, pl.ds(off, BLK)]
            acts = tok_ref[at, :]
            for c in range(3):
                raw = contract(wt[c * cols : (c + 1) * cols, :], acts, 1, 1)
                raw = raw + jnp.tile(bias[c * cols : (c + 1) * cols, :], (1, BLK // 128))
                if c == 2:
                    qkv_ref[2 * cols : 3 * cols, at] = raw.astype(LOW)
                    continue
                for h in range(heads):
                    first = raw[h * HD : h * HD + HALF]
                    second = raw[h * HD + HALF : (h + 1) * HD]
                    one = (first * cosine - second * sine).astype(LOW)
                    two = (second * cosine + first * sine).astype(LOW)
                    if c == 0:
                        one = one * jnp.asarray(HD**-0.5, LOW)
                        two = two * jnp.asarray(HD**-0.5, LOW)
                    base = c * cols + h * HD
                    qkv_ref[base : base + HALF, at] = one
                    qkv_ref[base + HALF : base + HD, at] = two
            return carry

        lax.fori_loop(0, blocks, project, 0)

    start, number = bounds_of(len_ref, count, block)
    start = pl.multiple_of(start, BLK)
    here = pl.ds(pl.multiple_of(block * BLK, BLK), BLK)

    def attend(n):
        for h in range(heads):
            query = qkv_ref[h * HD : (h + 1) * HD, here]
            slot = h % 2
            peak = jnp.full((8, BLK), -jnp.inf, F32)
            for k in range(n * BLK // TILE):
                near = qkv_ref[cols + h * HD : cols + (h + 1) * HD, pl.ds(start + k * TILE, TILE)]
                score = contract(near, query, 0, 0)
                s_scr[slot, k * TILE : (k + 1) * TILE, :] = score
                peak = jnp.maximum(peak, jnp.max(score.reshape(TILE // 8, 8, BLK), axis=0))
            peak = jnp.max(peak, axis=0, keepdims=True)
            total = jnp.zeros((8, BLK), F32)
            for k in range(n * BLK // TILE):
                expo = jnp.exp(s_scr[slot, k * TILE : (k + 1) * TILE, :] - peak)
                total = total + jnp.sum(expo.reshape(TILE // 8, 8, BLK), axis=0)
                pt_ref[0, h, k * TILE : (k + 1) * TILE, :] = expo.astype(LOW)
            inverse = 1.0 / jnp.sum(total, axis=0, keepdims=True)
            values = qkv_ref[2 * cols + h * HD : 2 * cols + (h + 1) * HD, pl.ds(start, n * BLK)]
            result = contract(values, pt_ref[0, h, 0 : n * BLK, :], 1, 0)
            ot_ref[h * HD : (h + 1) * HD, here] = result
            r_ref[h : h + 1, here] = inverse
            mix[h * HD : (h + 1) * HD, here] = (result * inverse).astype(LOW)

    for n in range(1, WINDOW + 1):
        pl.when(number == n)(functools.partial(attend, n))

    for c in range(NC):

        @pl.when(block == (c + 1) * (rows // BLK) // NC - 1)
        def _():
            for k, ref in enumerate((m0, m1, m2, m3)):
                owner = jnp.bitwise_xor(pos_ref[0], k)
                at = pl.multiple_of(c * (rows // NC) + owner * piece, 128)
                ref[:, c * piece : (c + 1) * piece] = mix[:, pl.ds(at, piece)]


def backward_kernel(
    count,
    len_ref,
    pos_ref,
    qkv_ref,
    pt_ref,
    ot_ref,
    r_ref,
    g0,
    g1,
    g2,
    g3,
    trig_ref,
    gp_ref,
    gb_ref,
    do_scr,
    delta,
    grads,
    ds_scr,
):
    block = pl.program_id(0)
    blocks = pl.num_programs(0)
    rows = qkv_ref.shape[1]
    cols = qkv_ref.shape[0] // 3
    heads = cols // HD
    piece = rows // (NC * 4)

    @pl.when(block == 0)
    def _():
        grads[cols : 3 * cols, :] = jnp.zeros((2 * cols, rows), F32)
        for k, ref in enumerate((g0, g1, g2, g3)):
            owner = jnp.bitwise_xor(pos_ref[0], k)
            for c in range(NC):
                at = pl.ds(pl.multiple_of(c * (rows // NC) + owner * piece, 128), piece)
                for h in range(heads):
                    inverse = r_ref[h : h + 1, at]
                    grad = ref[h * HD : (h + 1) * HD, c * piece : (c + 1) * piece]
                    grad = (grad.astype(F32) * inverse).astype(LOW)
                    do_scr[h * HD : (h + 1) * HD, at] = grad
                    mixed = ot_ref[h * HD : (h + 1) * HD, at]
                    dots = jnp.sum(grad.astype(F32) * mixed, axis=0, keepdims=True)
                    delta[h : h + 1, at] = dots * inverse

    start, number = bounds_of(len_ref, count, block)
    start = pl.multiple_of(start, BLK)
    here = pl.ds(pl.multiple_of(block * BLK, BLK), BLK)

    def attend(n):
        whole = pl.ds(start, n * BLK)
        for h in range(heads):
            slot = h % 2
            hs = h * HD
            grad = do_scr[hs : hs + HD, here]
            shift = delta[h : h + 1, here]
            for k in range(n * BLK // TILE):
                values = qkv_ref[2 * cols + hs : 2 * cols + hs + HD, pl.ds(start + k * TILE, TILE)]
                grad_p = contract(values, grad, 0, 0)
                prob = pt_ref[0, h, k * TILE : (k + 1) * TILE, :].astype(F32)
                ds_scr[slot, k * TILE : (k + 1) * TILE, :] = (prob * (grad_p - shift)).astype(LOW)
            grad_s = ds_scr[slot, 0 : n * BLK, :]
            grads[2 * cols + hs : 2 * cols + hs + HD, whole] += contract(
                grad, pt_ref[0, h, 0 : n * BLK, :], 1, 1
            )
            query = qkv_ref[hs : hs + HD, here]
            grads[cols + hs : cols + hs + HD, whole] += contract(query, grad_s, 1, 1)
            near = qkv_ref[cols + hs : cols + hs + HD, whole]
            grads[hs : hs + HD, here] = contract(near, grad_s, 1, 0) * (HD**-0.5)

    for n in range(1, WINDOW + 1):
        pl.when(number == n)(functools.partial(attend, n))

    @pl.when(block == blocks - 1)
    def _():
        gb_ref[...] = jnp.zeros_like(gb_ref)

        def finish(j, carry):
            begin, _ = bounds_of(len_ref, count, j)
            off = pl.multiple_of(j * BLK - begin, BLK)
            at = pl.ds(pl.multiple_of(j * BLK, BLK), BLK)
            cosine = trig_ref[0:HALF, pl.ds(off, BLK)]
            sine = trig_ref[HALF:HD, pl.ds(off, BLK)]

            def emit(base, size, value):
                gp_ref[base : base + size, at] = value.astype(LOW)
                part = value[:, 0:128]
                for i in range(1, BLK // 128):
                    part = part + value[:, i * 128 : (i + 1) * 128]
                gb_ref[base : base + size, :] += part

            for c in range(2):
                for h in range(heads):
                    base = c * cols + h * HD
                    first = grads[base : base + HALF, at]
                    second = grads[base + HALF : base + HD, at]
                    emit(base, HALF, first * cosine + second * sine)
                    emit(base + HALF, HALF, second * cosine - first * sine)
            emit(2 * cols, cols, grads[2 * cols : 3 * cols, at])
            return carry

        lax.fori_loop(0, blocks, finish, 0)


def resident(shape):
    return pl.BlockSpec(shape, lambda i, *_: (0,) * len(shape), pipeline_mode=pl.Buffered(1))


def kept(shape):
    return pl.BlockSpec(shape, lambda i, *_: (0,) * len(shape))


def attention_forward(lengths, place, tokens, weight, bias, trig):
    rows = tokens.shape[0]
    cols = weight.shape[2]
    heads = cols // HD
    blocks = rows // BLK
    share = rows // 4
    pairs = blocks * WINDOW * heads * BLK * BLK
    return pl.pallas_call(
        functools.partial(forward_kernel, lengths.shape[0]),
        name="attend_forward",
        grid_spec=pltpu.PrefetchScalarGridSpec(
            num_scalar_prefetch=2,
            grid=(blocks,),
            in_specs=[
                resident(tokens.shape),
                resident(weight.shape),
                resident(bias.shape),
                resident(trig.shape),
            ],
            out_specs=[
                kept((3 * cols, rows)),
                pl.BlockSpec((1, heads, SPAN, BLK), lambda i, *_: (i, 0, 0, 0)),
                kept((cols, rows)),
                kept((8, rows)),
            ]
            + [kept((cols, share))] * 4,
            scratch_shapes=[
                pltpu.VMEM((3 * cols, weight.shape[1]), LOW),
                pltpu.VMEM((3 * cols, 128), F32),
                pltpu.VMEM((2, SPAN, BLK), F32),
                pltpu.VMEM((cols, rows), LOW),
            ],
        ),
        out_shape=[
            jax.ShapeDtypeStruct((3 * cols, rows), LOW),
            jax.ShapeDtypeStruct((blocks, heads, SPAN, BLK), LOW),
            jax.ShapeDtypeStruct((cols, rows), F32),
            jax.ShapeDtypeStruct((8, rows), F32),
        ]
        + [jax.ShapeDtypeStruct((cols, share), LOW)] * 4,
        cost_estimate=pl.CostEstimate(
            flops=pairs * 4 * 256 + 2 * rows * 3 * cols * tokens.shape[1],
            bytes_accessed=pairs * 2 + 12_000_000,
            transcendentals=pairs,
        ),
    )(lengths, place, tokens, weight, bias, trig)


def attention_backward(lengths, place, qkv, probs, raw, inverse, grads, trig):
    rows = qkv.shape[1]
    cols = qkv.shape[0] // 3
    heads = cols // HD
    blocks = rows // BLK
    pairs = blocks * WINDOW * heads * BLK * BLK
    return pl.pallas_call(
        functools.partial(backward_kernel, lengths.shape[0]),
        name="attend_backward",
        grid_spec=pltpu.PrefetchScalarGridSpec(
            num_scalar_prefetch=2,
            grid=(blocks,),
            in_specs=[
                resident(qkv.shape),
                pl.BlockSpec((1, heads, SPAN, BLK), lambda i, *_: (i, 0, 0, 0)),
                resident(raw.shape),
                resident(inverse.shape),
            ]
            + [resident(g.shape) for g in grads]
            + [resident(trig.shape)],
            out_specs=[kept((3 * cols, rows)), kept((3 * cols, 128))],
            scratch_shapes=[
                pltpu.VMEM((cols, rows), LOW),
                pltpu.VMEM((8, rows), F32),
                pltpu.VMEM((3 * cols, rows), F32),
                pltpu.VMEM((2, SPAN, BLK), LOW),
            ],
        ),
        out_shape=[
            jax.ShapeDtypeStruct((3 * cols, rows), LOW),
            jax.ShapeDtypeStruct((3 * cols, 128), F32),
        ],
        cost_estimate=pl.CostEstimate(
            flops=pairs * 8 * 256, bytes_accessed=pairs * 2 + 12_000_000, transcendentals=0
        ),
    )(lengths, place, qkv, probs, raw, inverse, *grads, trig)


def swap(value, axis, mask):
    size = lax.axis_size(axis)
    return lax.ppermute(value, axis, [(i, i ^ mask) for i in range(size)])


def half_of(value, bit):
    half = value.shape[0] // 2
    return lax.dynamic_slice_in_dim(value, bit * half, half, 0)


def scatter_sum(value, axis, order):
    index = lax.axis_index(axis)
    for mask in order:
        bit = (index & mask) // mask
        got = swap(half_of(value, 1 - bit), axis, mask)
        value = (half_of(value, bit).astype(F32) + got.astype(F32)).astype(LOW)
    return value


def gather_back(value, axis, order):
    index = lax.axis_index(axis)
    for mask in reversed(order):
        bit = (index & mask) // mask
        got = swap(value, axis, mask)
        value = jnp.where(
            bit == 0,
            jnp.concatenate([value, got], axis=0),
            jnp.concatenate([got, value], axis=0),
        )
    return value


def masks_of(size):
    masks = []
    mask = 1
    while mask < size:
        masks.append(mask)
        mask = mask * 2
    return masks


def rotated(masks, by):
    by = by % max(len(masks), 1)
    return masks[by:] + masks[:by]


def spread(pieces, place, dtype):
    chunks, size, width = pieces[0].shape
    whole = jnp.zeros((chunks, 4, size, width), dtype)
    for k, piece in enumerate(pieces):
        whole = lax.dynamic_update_slice(
            whole, piece.astype(dtype)[:, None], (0, place ^ k, 0, 0)
        )
    return whole.reshape(chunks * 4 * size, width)


def on_device(
    tokens,
    cotangent,
    doc_lengths,
    qkv_weight,
    qkv_bias,
    out_weight,
    out_bias,
    up_weight,
    up_bias,
    down_weight,
    down_bias,
    norm_gains,
    norm_shifts,
):
    rows, width = tokens.shape
    cols = qkv_weight.shape[2]
    hidden_dev = up_weight.shape[1]
    groups = lax.axis_size("dp")
    factor = 1.0 / math.sqrt(rows * groups)
    place = lax.axis_index("tensor").astype(jnp.int32)
    core = place & 1
    piece = rows // (NC * 4)
    share = rows // 4
    masks = masks_of(groups)
    trig = jnp.asarray(trig_table())
    lengths = doc_lengths[0]
    where = place.reshape(1)

    def gathered(value):
        far = swap(value, "tensor", 2)
        return [value, swap(value, "tensor", 1), far, swap(far, "tensor", 1)]

    out_w = gathered(out_weight)
    up_w = gathered(up_weight)
    up_b = gathered(up_bias[None])
    down_w = gathered(down_weight)

    def own(value):
        cut = value.reshape(NC, 4, piece, width)
        return lax.dynamic_slice_in_dim(cut, place, 1, 1).reshape(share, width)

    qkv, probs, raw, inverse, *mixed = attention_forward(
        lengths, where, tokens, qkv_weight, qkv_bias, trig
    )
    mixed = [mixed[0]] + [swap(mixed[k], "tensor", k) for k in range(1, 4)]
    mixed_t = jnp.concatenate(mixed, axis=0)
    out_all = jnp.concatenate(out_w, axis=0)
    attn = contract(mixed_t, out_all, 0, 0)
    first_sum = own(tokens).astype(F32) + attn + out_bias
    unit_one, inverse_one = normalize(first_sum)
    hidden = unit_one * norm_gains[0] + norm_shifts[0]
    hidden_low = hidden.astype(LOW)
    pre = [contract(hidden_low, up_w[k], 1, 0) + up_b[k] for k in range(4)]
    active = [gelu_value(p).astype(LOW) for p in pre]
    ffn = contract(jnp.concatenate(active, axis=1), jnp.concatenate(down_w, axis=0), 1, 0)
    second_sum = hidden + ffn + down_bias
    unit_two, inverse_two = normalize(second_sum)
    output_own = (unit_two * norm_gains[1] + norm_shifts[1]).astype(LOW)
    grad_out = own(cotangent).astype(F32)
    gain_two_grad = jnp.sum(grad_out * unit_two, axis=0)
    shift_two_grad = jnp.sum(grad_out, axis=0)
    grad_second = normalize_back(grad_out, unit_two, inverse_two, norm_gains[1])
    down_bias_grad = jnp.sum(grad_second, axis=0)
    grad_ffn = grad_second.astype(LOW)
    grad_pre = [contract(grad_ffn, down_w[k], 1, 1) * gelu_slope(pre[k]) for k in range(4)]
    grad_pre_low = [g.astype(LOW) for g in grad_pre]
    hidden_grad = grad_second + contract(
        jnp.concatenate(grad_pre_low, axis=1), jnp.concatenate(up_w, axis=1), 1, 1
    )
    gain_one_grad = jnp.sum(hidden_grad * unit_one, axis=0)
    shift_one_grad = jnp.sum(hidden_grad, axis=0)
    grad_first = normalize_back(hidden_grad, unit_one, inverse_one, norm_gains[0])
    out_bias_grad = jnp.sum(grad_first, axis=0)
    grad_attn = grad_first.astype(LOW)
    grad_mixed = [contract(out_w[k], grad_attn, 1, 1).astype(LOW) for k in range(4)]
    grad_mixed = [grad_mixed[0]] + [swap(grad_mixed[k], "tensor", k) for k in range(1, 4)]

    down_grad = [contract(active[k], grad_ffn, 0, 0).astype(LOW) for k in range(4)]
    up_grad = [contract(hidden_low, grad_pre_low[k], 0, 0).astype(LOW) for k in range(4)]
    out_grad = [contract(mixed[k], grad_attn, 1, 0) for k in range(4)]
    small = [out_bias_grad, down_bias_grad, gain_one_grad, gain_two_grad, shift_one_grad, shift_two_grad]
    rest_grad = [
        jnp.concatenate(
            [out_grad[k], jnp.sum(grad_pre[k], axis=0)[None]]
            + [s[None] for s in small]
            + [jnp.zeros((57, width), F32)],
            axis=0,
        ).astype(LOW)
        for k in range(4)
    ]

    def to_owner(parts):
        near = parts[0].astype(F32) + swap(parts[1], "tensor", 1).astype(F32)
        far = parts[2].astype(F32) + swap(parts[3], "tensor", 1).astype(F32)
        near = near.astype(LOW)
        return (near.astype(F32) + swap(far.astype(LOW), "tensor", 2).astype(F32)).astype(LOW)

    def reduced(value, turn):
        order = rotated(masks, turn)
        mine = scatter_sum(value, "dp", order)
        mine = (mine.astype(F32) * factor).astype(LOW)
        return gather_back(mine, "dp", order).astype(F32)

    down_done = reduced(to_owner(down_grad), 0)
    up_done = reduced(to_owner(up_grad), 1)
    rest_done = reduced(to_owner(rest_grad), 0)

    far_out = swap(output_own, "tensor", 2)
    out_pieces = [output_own, swap(output_own, "tensor", 1), far_out, swap(far_out, "tensor", 1)]
    output = spread([p.reshape(NC, piece, width) for p in out_pieces], place, LOW)

    grad_proj, bias_part = attention_backward(
        lengths, where, qkv, probs, raw, inverse, grad_mixed, trig
    )
    input_part = contract(
        grad_proj, jnp.swapaxes(qkv_weight, 1, 2).reshape(3 * cols, width), 0, 0
    ).astype(LOW)
    cut = input_part.reshape(NC, 2, 2, piece, width)
    kept_half = lax.dynamic_slice_in_dim(cut, core, 1, 2)[:, :, 0]
    sent_half = lax.dynamic_slice_in_dim(cut, 1 - core, 1, 2)[:, :, 0]
    both = kept_half.astype(F32) + swap(sent_half, "tensor", 1).astype(F32)
    mine = (lax.broadcasted_iota(jnp.int32, (1, 2, 1, 1), 1) == place // 2)
    both = both + jnp.where(mine, grad_first.reshape(NC, 1, piece, width), 0.0)
    both = both.astype(LOW)
    both = (both.astype(F32) + swap(both, "tensor", 2).astype(F32)).astype(LOW)
    other = swap(both, "tensor", 1)
    pair = jnp.where(
        core == 0, jnp.stack([both, other], axis=2), jnp.stack([other, both], axis=2)
    )
    input_grad = pair.astype(F32).reshape(rows, width)

    qkv_grad = contract(grad_proj, tokens, 1, 0).astype(LOW)
    bias_row = jnp.pad(jnp.sum(bias_part, axis=1), (0, width - 3 * cols))[None].astype(LOW)
    qkv_flat = jnp.concatenate(
        [qkv_grad, bias_row, jnp.zeros((63, width), LOW)], axis=0
    )
    qkv_done = reduced(qkv_flat, 1)
    qkv_weight_grad = jnp.swapaxes(qkv_done[: 3 * cols].reshape(3, cols, width), 1, 2)
    qkv_bias_grad = qkv_done[3 * cols, : 3 * cols].reshape(3, cols)
    return (
        output,
        input_grad,
        qkv_weight_grad,
        qkv_bias_grad,
        rest_done[:cols],
        rest_done[cols + 1],
        up_done,
        rest_done[cols],
        down_done,
        rest_done[cols + 2],
        rest_done[cols + 3 : cols + 5],
        rest_done[cols + 5 : cols + 7],
    )


def solution(mesh):
    return jax.shard_map(
        on_device,
        mesh=mesh,
        in_specs=(
            P("dp", None),
            P("dp", None),
            P("dp", None),
            P(None, None, "tensor"),
            P(None, "tensor"),
            P("tensor", None),
            P(),
            P(None, "tensor"),
            P("tensor"),
            P("tensor", None),
            P(),
            P(),
            P(),
        ),
        out_specs=(
            P("dp", None),
            P("dp", None),
            P(None, None, "tensor"),
            P(None, "tensor"),
            P("tensor", None),
            P(),
            P(None, "tensor"),
            P("tensor"),
            P("tensor", None),
            P(),
            P(),
            P(),
        ),
        check_vma=False,
    )
```
